256 devices in a mesh: expert: 4 (over x_lo, core), hidden: 64 (over y, x_hi, z).
Axes of the slice: x: 4 (x_hi: 2, x_lo: 2; x = x_hi * 2 + x_lo), y: 4, z: 8, core: 2. Of those that a mesh axis runs over, the one named last changes fastest.
Arguments:
- tokens: bfloat16 [512, 6144], P(('expert', 'hidden')), may hold values from -6 to 6
- routing: int32 [512, 2], P(('expert', 'hidden')), may hold values from 0 to 3, all different within a row; in each aligned block of 2 rows (0 to 1, 2 to 3, ...) at most 2 rows name the same one
- mix_weights: float32 [512, 2], P(('expert', 'hidden')), may hold values from 0.2 to 1
- gate_weight: bfloat16 [4, 6144, 16384], P('expert', None, 'hidden'), may hold values from -0.078125 to 0.078125
- up_weight: bfloat16 [4, 6144, 16384], P('expert', None, 'hidden'), may hold values from -0.078125 to 0.078125
- down_weight: bfloat16 [4, 16384, 6144], P('expert', 'hidden'), may hold values from -0.125 to 0.125
Outputs:
- mixed: bfloat16 [512, 6144], P(('expert', 'hidden'))
The draws below stay inside these ranges and needn't reach their ends.
Inputs may be any that keep to these rules, and one draw needn't show every extreme that they name: `routing`: each row names two different experts. Within each aligned block of 2 rows (the tokens of one device) no expert is named by more than 2 entries, and in every draw some expert is named by exactly 2 entries of some block.
All inputs are finite; a program needn't handle non-finite values.
Results may differ from the reference program's by a relative error of at most 0.0058.
Values may be sent and summed in bfloat16 or wider, within the bound.
No kernel may reach another device: no remote copies, remote signals or barrier semaphores. Data moves between devices by JAX's collectives and lax.ppermute only.
A program may use at most 128 MiB of HBM per device.

```python
import math
import jax
import jax.numpy as jnp
import numpy as np
from jax import lax

D = 6144
FF = 16384
TOK_DEV = 2
CAP = 2
EXPERTS = 4
TOKENS = 512


def spiked(values, own_key, source, target, parts, factor):
    owner, partner = [(jnp.arange(values.shape[axis_at]) // (values.shape[axis_at] // parts)).reshape([-1 if axis == axis_at else 1 for axis in range(values.ndim)]) for axis_at in (source, target)]
    chosen = jax.random.permutation(own_key, parts)[partner]
    strong = (owner == chosen) | (owner == (partner + parts // 2) % parts)
    return jnp.where(strong, factor * values, values)


def block_levels(own_key, extent, cuts, low, largest):
    level = 1.0
    for dim, parts in cuts:
        steps = jax.random.uniform(jax.random.fold_in(jax.random.fold_in(own_key, 6), dim), (parts,), jnp.float32, low / len(cuts), largest / len(cuts))
        level = level * jnp.repeat(jnp.exp(steps), extent[dim] // parts).reshape((-1,) + (1,) * (len(extent) - 1 - dim))
    return level


def assign_block(own_key, own, number, rows, amount, top, reach, lean):
    sequence = jax.random.permutation(own_key, amount)
    crowded, common = shares(amount, rows * top, reach, lean, True), shares(amount, rows * top, reach, lean, False)
    places = jnp.arange(amount)

    def named(sizes, turn):
        used = int((sizes > 0).sum())
        fixed = max(1, used // 4)
        shifted = fixed + (places - fixed + turn * (used - fixed)) % max(1, amount - fixed)
        return jnp.zeros((amount,), jnp.int32).at[sequence[jnp.where(places < fixed, places, shifted)]].set(jnp.asarray(sizes, jnp.int32))

    sizes = jnp.where(number % 4 == 0, named(crowded, number // 4), named(common, number - number // 4 - 1))
    mixed = jax.random.permutation(jax.random.fold_in(own, 3), amount)
    giver, receiver = mixed[0:amount // 2 * 2:2], mixed[1:amount // 2 * 2:2]
    slack = jnp.minimum(sizes[giver] - 1, reach - sizes[receiver]) // 2
    slack = jnp.where((giver == sequence[0]) | (receiver == sequence[0]) | (sizes[receiver] == 0), 0, jnp.maximum(slack, 0))
    shifted = jax.random.randint(jax.random.fold_in(own, 4), (amount // 2,), 0, 1 << 20) % (slack + 1)
    sizes = sizes.at[giver].add(-shifted).at[receiver].add(shifted)
    members = jnp.searchsorted(jnp.cumsum(sizes), jnp.arange(rows * top), side="right").astype(jnp.int32)
    grid = members.reshape(top, rows).T
    grid = grid[jax.random.permutation(jax.random.fold_in(own, 1), rows)]
    turn = jax.random.randint(jax.random.fold_in(own, 2), (rows, 1), 0, top)
    return jnp.take_along_axis(grid, (jnp.arange(top)[None, :] + turn) % top, axis=1)


def shares(number_of, total, bound, skew, full):
    loads = [(1 << 20) // math.isqrt(rank ** skew) + 1 for rank in range(1, number_of + 1)]
    largest = bound if full else min(bound, max(-(-total // number_of), total * loads[0] // sum(loads)))
    least = 1 if total - largest >= number_of - 1 else 0
    holding, surplus = [largest] + [least] * (number_of - 1), total - largest - least * (number_of - 1)
    while surplus > 0:
        free = [i for i in range(1, number_of) if holding[i] < largest] or [i for i in range(1, number_of) if holding[i] < bound]
        whole, budget = sum([loads[i] for i in free]), surplus
        for i in free:
            addition = min(bound - holding[i], max(1, budget * loads[i] // whole), surplus)
            holding[i] = holding[i] + addition
            surplus = surplus - addition
    return np.array(holding)


def gaussian(key, dims, scale, most, pieces=(), kind=jnp.bfloat16):
    values = scale * jax.random.normal(key, dims, jnp.float32)
    if pieces:
        values = values * block_levels(key, dims, pieces, -0.22, 0.18)
    return jnp.clip(values, -most, most).astype(kind)


def heavy_noise(own_key, extent, width, most, pieces, heavy, kind=jnp.bfloat16):
    values = width * jax.random.normal(own_key, extent, jnp.float32)
    if pieces:
        values = values * block_levels(own_key, extent, pieces, -0.22, 0.18)
    return jnp.clip(spiked(values, jax.random.fold_in(own_key, 3), *heavy), -most, most).astype(kind)


def setup_inputs(seed: int = 0) -> dict:
    key_list = jax.random.split(jax.random.key(seed), 7)
    tokens = gaussian(key_list[0], (TOKENS, D), 1.0, 6.0, ((0, 256),))
    routing_keys = jax.random.split(jax.random.fold_in(key_list[1], 1), TOKENS // TOK_DEV)
    routing_turns = jax.random.permutation(jax.random.fold_in(key_list[1], 3), TOKENS // TOK_DEV)
    routing = jax.vmap(lambda own, number: assign_block(jax.random.fold_in(key_list[1], 2), own, number, TOK_DEV, EXPERTS, 2, CAP, 1))(routing_keys, routing_turns).reshape((TOKENS, 2))
    mix_weights = jnp.clip(0.2 + 0.8 * jax.random.uniform(key_list[2], (TOKENS, 2), jnp.float32) ** block_levels(key_list[2], (TOKENS, 2), ((0, 256),), -0.2, 0.2), 0.2, 1.0)
    gate_weight = gaussian(key_list[3], (EXPERTS, D, FF), D ** -0.5, 0.078125, ((0, 4), (2, 64)))
    up_weight = gaussian(key_list[4], (EXPERTS, D, FF), D ** -0.5, 0.078125, ((0, 4), (2, 64)))
    down_weight = heavy_noise(key_list[5], (EXPERTS, FF, D), FF ** -0.5, 0.125, ((0, 4), (1, 64)), (1, 2, 64, 4.0))
    return {"tokens": tokens, "routing": routing, "mix_weights": mix_weights, "gate_weight": gate_weight, "up_weight": up_weight, "down_weight": down_weight}


def reference(tokens, routing, mix_weights, gate_weight, up_weight, down_weight):
    blocks = TOKENS // TOK_DEV
    entries = routing.reshape(blocks, 2 * TOK_DEV).astype(jnp.int32)
    one_hot = (entries[:, :, None] == jnp.arange(EXPERTS, dtype=jnp.int32)[None, None, :]).astype(jnp.int32)
    earlier = (jnp.cumsum(one_hot, axis=1) - one_hot).astype(jnp.int32)
    slot_ids = jnp.sum(earlier * one_hot, axis=2).astype(jnp.int32)
    places = (jnp.arange(blocks, dtype=jnp.int32)[:, None] * CAP + slot_ids).reshape(-1).astype(jnp.int32)
    experts_flat = entries.reshape(-1)
    token_ids = (jnp.arange(TOKENS * 2, dtype=jnp.int32) // 2).astype(jnp.int32)
    padded = jnp.concatenate([tokens, jnp.zeros((1, D), tokens.dtype)], axis=0)

    def one_expert(expert):
        owners = jnp.where(experts_flat == expert, places, blocks * CAP).astype(jnp.int32)
        source_ids = jnp.full((blocks * CAP,), TOKENS, jnp.int32).at[owners].set(token_ids, mode="drop")
        expert_in = padded[source_ids]
        gate_out = jnp.dot(expert_in, gate_weight[expert], preferred_element_type=jnp.float32)
        up_out = jnp.dot(expert_in, up_weight[expert], preferred_element_type=jnp.float32)
        hidden = (jax.nn.silu(gate_out) * up_out).astype(jnp.bfloat16)
        return jnp.dot(hidden, down_weight[expert], preferred_element_type=jnp.float32).astype(jnp.bfloat16)

    expert_out = lax.map(one_expert, jnp.arange(EXPERTS, dtype=jnp.int32))
    picked = expert_out[experts_flat, places].astype(jnp.float32).reshape(TOKENS, 2, D)
    result = jnp.sum(mix_weights[:, :, None] * picked, axis=1)
    return result.astype(jnp.bfloat16)
```

```python
import jax
import jax.numpy as jnp
from jax import lax
from jax.sharding import Mesh
from jax.sharding import PartitionSpec as P

AXES = ("xl", "c", "y", "xh", "z")
SIZES = (2, 2, 4, 2, 8)
RING = 4
PAD = 128


def flat(xl, c, y, xh, z):
    return (((xl * 2 + c) * 4 + y) * 2 + xh) * 8 + z


def ring_perm(first, step):
    pairs = []
    for c in range(2):
        along_x = (c == 0) == first
        for x in range(4):
            for y in range(4):
                for z in range(8):
                    tx, ty = ((x + step) % 4, y) if along_x else (x, (y + step) % 4)
                    pairs.append((flat(x % 2, c, y, x // 2, z), flat(tx % 2, c, ty, tx // 2, z)))
    return pairs


def move(v, first, step):
    return lax.ppermute(v, AXES, ring_perm(first, step))


def swap(v):
    return lax.ppermute(v, "c", [(0, 1), (1, 0)])


def ring_gather(block, first):
    half = block.shape[0] // 2
    one, two = block[:half], block[half:]
    from_left_one = move(one, first, 1)
    from_right_two = move(two, first, -1)
    from_left_two = move(two, first, 1)
    from_right_one = move(one, first, -1)
    far_one = move(from_left_one, first, 1)
    far_two = move(from_right_two, first, -1)
    return [one, two, from_right_one, from_right_two, far_one, far_two, from_left_one, from_left_two]


def add(*terms):
    total = terms[0].astype(jnp.float32)
    for term in terms[1:]:
        total = total + term.astype(jnp.float32)
    return total


def ring_reduce(blocks, first):
    own, right, far, left = blocks
    half = own.shape[0] // 2
    to_right = move(far[:half], first, 1)
    to_left = move(far[half:], first, -1)
    right_two = move(right[half:], first, 1)
    left_one = move(left[:half], first, -1)
    right_one = move(add(right[:half], to_right).astype(jnp.bfloat16), first, 1)
    left_two = move(add(left[half:], to_left).astype(jnp.bfloat16), first, -1)
    one = add(own[:half], right_one, left_one)
    two = add(own[half:], right_two, left_two)
    return jnp.concatenate([one, two], axis=0)


def parts(w):
    high = lax.reduce_precision(w, 8, 7)
    mid = lax.reduce_precision(w - high, 8, 7)
    low = w - high - mid
    return jnp.concatenate([high, mid, low], axis=1).astype(jnp.bfloat16)


def shards(tokens, routing, mix_weights, gate_weight, up_weight, down_weight):
    tok_rows, width = tokens.shape
    half = width // 2
    core = lax.axis_index("c")
    expert = lax.axis_index("xl") * 2 + core
    experts = jnp.arange(4, dtype=jnp.int32)
    chosen = routing[:, :, None] == experts[None, None, :]
    share = jnp.sum(jnp.where(chosen, mix_weights[:, :, None], 0.0), axis=1)
    extra = jnp.pad(parts(share), ((0, 0), (0, PAD - 12)))
    sides = [jnp.concatenate([tokens[:, i * half:(i + 1) * half], extra], axis=1) for i in range(2)]
    outgoing = jnp.stack([sides[0]] * 8 + [sides[1]] * 8, axis=0)
    tile = lax.all_to_all(outgoing, ("c", "z"), split_axis=0, concat_axis=0, tiled=True)
    tile = tile.reshape(16 * tok_rows, half + PAD)
    rows = tile.shape[0]
    quarter = jnp.concatenate(ring_gather(tile, True), axis=0)
    quarter = quarter.reshape(RING, rows, half + PAD)
    pieces = ring_gather(quarter, False)
    mine = jnp.concatenate(pieces, axis=0)
    other = swap(mine)

    def halves(w, axis):
        own = lax.dynamic_slice_in_dim(w, core * half, half, axis)
        rest = lax.dynamic_slice_in_dim(w, (1 - core) * half, half, axis)
        return own, rest

    w_in = jnp.concatenate([gate_weight[0], up_weight[0]], axis=1)
    in_own, in_rest = [jnp.pad(w, ((0, PAD), (0, 0))) for w in halves(w_in, 0)]
    down_own, down_rest = halves(down_weight[0], 1)
    n = RING * RING * rows
    units = gate_weight.shape[2]

    def turned(v):
        return v.reshape(RING, RING, rows, v.shape[-1]).swapaxes(0, 1).reshape(n, v.shape[-1])

    mine = mine.reshape(n, half + PAD)
    other = other.reshape(n, half + PAD)
    act = jnp.dot(mine, in_own, preferred_element_type=jnp.float32)
    act = act + turned(jnp.dot(other, in_rest, preferred_element_type=jnp.float32))
    hidden = (jax.nn.silu(act[:, :units]) * act[:, units:]).astype(jnp.bfloat16)
    hidden_rest = turned(hidden)

    lane = jnp.arange(PAD, dtype=jnp.int32)
    mask = (lane % 4 == expert) & (lane < 12)

    def scale_of(v):
        return jnp.sum(jnp.where(mask[None, :], v[:, half:].astype(jnp.float32), 0.0), axis=1, keepdims=True)

    scale_own, scale_rest = scale_of(mine), scale_of(other)
    per = n // RING
    blocks = [None] * RING
    for d in (2, 1, 3, 0):
        span = slice(d * per, (d + 1) * per)
        rest = jnp.dot(hidden_rest[span], down_rest, preferred_element_type=jnp.float32) * scale_rest[span]
        came = swap(rest.astype(jnp.bfloat16))
        own = jnp.dot(hidden[span], down_own, preferred_element_type=jnp.float32) * scale_own[span]
        blocks[d] = add(own, came).astype(jnp.bfloat16).reshape(RING, rows, half)
    summed = ring_reduce(blocks, False).astype(jnp.bfloat16)
    last = ring_reduce([summed[d] for d in range(RING)], True)
    back = lax.all_to_all(last.reshape(16, tok_rows, half), ("c", "z"), split_axis=0, concat_axis=0, tiled=True)
    total = jnp.sum(back.reshape(2, 8, tok_rows, half), axis=1)
    return jnp.concatenate([total[0], total[1]], axis=1).astype(jnp.bfloat16)


def solution(mesh):
    fine = Mesh(mesh.devices.reshape(SIZES), AXES)
    expert, hidden = ("xl", "c"), ("y", "xh", "z")
    in_specs = (
        P(AXES, None),
        P(AXES, None),
        P(AXES, None),
        P(expert, None, hidden),
        P(expert, None, hidden),
        P(expert, hidden, None),
    )
    return jax.shard_map(shards, mesh=fine, in_specs=in_specs, out_specs=P(AXES, None), check_vma=False)
```

```python
import jax
import jax.numpy as jnp
from jax import lax
from jax.sharding import Mesh
from jax.sharding import PartitionSpec as P

AXES = ("xl", "c", "y", "xh", "z")
SIZES = (2, 2, 4, 2, 8)
RING = 4
PAD = 128


def flat(xl, c, y, xh, z):
    return (((xl * 2 + c) * 4 + y) * 2 + xh) * 8 + z


def ring_perm(first, step):
    pairs = []
    for c in range(2):
        along_x = (c == 0) == first
        for x in range(4):
            for y in range(4):
                for z in range(8):
                    tx, ty = ((x + step) % 4, y) if along_x else (x, (y + step) % 4)
                    pairs.append((flat(x % 2, c, y, x // 2, z), flat(tx % 2, c, ty, tx // 2, z)))
    return pairs


def move(v, first, step):
    return lax.ppermute(v, AXES, ring_perm(first, step))


def swap(v):
    return lax.ppermute(v, "c", [(0, 1), (1, 0)])


def ring_gather(one, two, first):
    from_left_one = move(one, first, 1)
    from_right_two = move(two, first, -1)
    from_left_two = move(two, first, 1)
    from_right_one = move(one, first, -1)
    far_one = move(from_left_one, first, 1)
    far_two = move(from_right_two, first, -1)
    return [one, two, from_right_one, from_right_two, far_one, far_two, from_left_one, from_left_two]


def add(*terms):
    total = terms[0].astype(jnp.float32)
    for term in terms[1:]:
        total = total + term.astype(jnp.float32)
    return total


def ring_reduce(blocks, first):
    own, right, far, left = blocks
    half = own.shape[0] // 2
    to_right = move(far[:half], first, 1)
    to_left = move(far[half:], first, -1)
    right_two = move(right[half:], first, 1)
    left_one = move(left[:half], first, -1)
    right_one = move(add(right[:half], to_right).astype(jnp.bfloat16), first, 1)
    left_two = move(add(left[half:], to_left).astype(jnp.bfloat16), first, -1)
    one = add(own[:half], right_one, left_one)
    two = add(own[half:], right_two, left_two)
    return one, two


def parts(w):
    high = lax.reduce_precision(w, 8, 7)
    mid = lax.reduce_precision(w - high, 8, 7)
    low = w - high - mid
    return jnp.concatenate([high, mid, low], axis=1).astype(jnp.bfloat16)


def shards(tokens, routing, mix_weights, gate_weight, up_weight, down_weight):
    tok_rows, width = tokens.shape
    half = width // 2
    core = lax.axis_index("c")
    expert = lax.axis_index("xl") * 2 + core
    experts = jnp.arange(4, dtype=jnp.int32)
    chosen = routing[:, :, None] == experts[None, None, :]
    share = jnp.sum(jnp.where(chosen, mix_weights[:, :, None], 0.0), axis=1)
    extra = jnp.pad(parts(share), ((0, 0), (0, PAD - 12)))
    sides = [jnp.concatenate([tokens[:, i * half:(i + 1) * half], extra], axis=1) for i in range(2)]
    outgoing = jnp.stack([sides[0]] * 8 + [sides[1]] * 8, axis=0)
    tile = lax.all_to_all(outgoing, ("c", "z"), split_axis=0, concat_axis=0, tiled=True)
    tile = tile.reshape(16 * tok_rows, half + PAD)
    rows = tile.shape[0]
    tiles = [tile] + [move(tile, True, step) for step in (-1, 2, 1)]
    one = jnp.stack(tiles[:2], axis=0)
    two = jnp.stack(tiles[2:], axis=0)
    mine = [v.reshape(2 * rows, half + PAD) for v in ring_gather(one, two, False)]
    other = [swap(v) for v in mine]

    def halves(w, axis):
        own = lax.dynamic_slice_in_dim(w, core * half, half, axis)
        rest = lax.dynamic_slice_in_dim(w, (1 - core) * half, half, axis)
        return own, rest

    w_in = jnp.concatenate([gate_weight[0], up_weight[0]], axis=1)
    in_own, in_rest = [jnp.pad(w, ((0, PAD), (0, 0))) for w in halves(w_in, 0)]
    down_own, down_rest = halves(down_weight[0], 1)
    n = RING * RING * rows
    units = gate_weight.shape[2]

    def turned(v):
        return v.reshape(RING, RING, rows, v.shape[-1]).swapaxes(0, 1).reshape(n, v.shape[-1])

    def product(pieces, w):
        return jnp.concatenate([jnp.dot(v, w, preferred_element_type=jnp.float32) for v in pieces], axis=0)

    act = product(mine, in_own) + turned(product(other, in_rest))
    hidden = (jax.nn.silu(act[:, :units]) * act[:, units:]).astype(jnp.bfloat16)
    hidden_rest = turned(hidden)

    lane = jnp.arange(PAD, dtype=jnp.int32)
    mask = (lane % 4 == expert) & (lane < 12)

    def scale_of(pieces):
        v = jnp.concatenate([p[:, half:] for p in pieces], axis=0)
        return jnp.sum(jnp.where(mask[None, :], v.astype(jnp.float32), 0.0), axis=1, keepdims=True)

    scale_own, scale_rest = scale_of(mine), scale_of(other)
    per = n // RING
    blocks = [None] * RING
    for d in (2, 1, 3, 0):
        span = slice(d * per, (d + 1) * per)
        rest = jnp.dot(hidden_rest[span], down_rest, preferred_element_type=jnp.float32) * scale_rest[span]
        came = swap(rest.astype(jnp.bfloat16))
        own = jnp.dot(hidden[span], down_own, preferred_element_type=jnp.float32) * scale_own[span]
        blocks[d] = add(own, came).astype(jnp.bfloat16).reshape(RING, rows, half)
    one, two = ring_reduce(blocks, False)
    from_left = move(one[1].astype(jnp.bfloat16), True, 1)
    from_far = move(two[0].astype(jnp.bfloat16), True, 2)
    from_right = move(two[1].astype(jnp.bfloat16), True, -1)
    last = add(one[0], from_left, from_far, from_right).astype(jnp.bfloat16)
    back = lax.all_to_all(last.reshape(16, tok_rows, half), ("c", "z"), split_axis=0, concat_axis=0, tiled=True)
    total = jnp.sum(back.reshape(2, 8, tok_rows, half).astype(jnp.float32), axis=1)
    return jnp.concatenate([total[0], total[1]], axis=1).astype(jnp.bfloat16)


def solution(mesh):
    fine = Mesh(mesh.devices.reshape(SIZES), AXES)
    expert, hidden = ("xl", "c"), ("y", "xh", "z")
    in_specs = (
        P(AXES, None),
        P(AXES, None),
        P(AXES, None),
        P(expert, None, hidden),
        P(expert, None, hidden),
        P(expert, hidden, None),
    )
    return jax.shard_map(shards, mesh=fine, in_specs=in_specs, out_specs=P(AXES, None), check_vma=False)
```

```python
import jax
import jax.numpy as jnp
from jax import lax
from jax.sharding import Mesh
from jax.sharding import PartitionSpec as P


AXES = ("xl", "c", "y", "xh", "z")
SIZES = (2, 2, 4, 2, 8)
RING = 4
PAD = 128


def flat(xl, c, y, xh, z):
    return (((xl * 2 + c) * 4 + y) * 2 + xh) * 8 + z


def ring_perm(first, step):
    pairs = []
    for c in range(2):
        along_x = (c == 0) == first
        for x in range(4):
            for y in range(4):
                for z in range(8):
                    tx, ty = ((x + step) % 4, y) if along_x else (x, (y + step) % 4)
                    pairs.append((flat(x % 2, c, y, x // 2, z), flat(tx % 2, c, ty, tx // 2, z)))
    return pairs


def move(v, first, step):
    return lax.ppermute(v, AXES, ring_perm(first, step))


def swap(v):
    return lax.ppermute(v, "c", [(0, 1), (1, 0)])


def ring_gather(one, two, first):
    from_left_one = move(one, first, 1)
    from_right_two = move(two, first, -1)
    from_left_two = move(two, first, 1)
    from_right_one = move(one, first, -1)
    far_one = move(from_left_one, first, 1)
    far_two = move(from_right_two, first, -1)
    return [one, two, from_right_one, from_right_two, from_left_one, from_left_two, far_one, far_two]


def add(*terms):
    total = terms[0].astype(jnp.float32)
    for term in terms[1:]:
        total = total + term.astype(jnp.float32)
    return total


def ring_reduce(blocks, first):
    own, right, left, far = blocks
    half = own.shape[0] // 2
    to_right = move(far[:half], first, 1)
    to_left = move(far[half:], first, -1)
    right_two = move(right[half:], first, 1)
    left_one = move(left[:half], first, -1)
    right_one = move(add(right[:half], to_right).astype(jnp.bfloat16), first, 1)
    left_two = move(add(left[half:], to_left).astype(jnp.bfloat16), first, -1)
    one = add(own[:half], right_one, left_one)
    two = add(own[half:], right_two, left_two)
    return one, two


def parts(w):
    high = lax.reduce_precision(w, 8, 7)
    mid = lax.reduce_precision(w - high, 8, 7)
    low = w - high - mid
    return jnp.concatenate([high, mid, low], axis=1).astype(jnp.bfloat16)


def shards(tokens, routing, mix_weights, gate_weight, up_weight, down_weight):
    tok_rows, width = tokens.shape
    half = width // 2
    core = lax.axis_index("c")
    expert = lax.axis_index("xl") * 2 + core
    experts = jnp.arange(4, dtype=jnp.int32)
    chosen = routing[:, :, None] == experts[None, None, :]
    share = jnp.sum(jnp.where(chosen, mix_weights[:, :, None], 0.0), axis=1)
    extra = jnp.pad(parts(share), ((0, 0), (0, PAD - 12)))
    sides = [jnp.concatenate([tokens[:, i * half:(i + 1) * half], extra], axis=1) for i in range(2)]
    outgoing = jnp.broadcast_to(jnp.stack(sides)[:, None], (2, 8) + sides[0].shape).reshape((16,) + sides[0].shape)
    tile = lax.all_to_all(outgoing, ("c", "z"), split_axis=0, concat_axis=0, tiled=True)
    tile = tile.reshape(16 * tok_rows, half + PAD)
    rows = tile.shape[0]

    def halves(w, axis):
        own = lax.dynamic_slice_in_dim(w, core * half, half, axis)
        rest = lax.dynamic_slice_in_dim(w, (1 - core) * half, half, axis)
        return own, rest

    w_in = jnp.concatenate([gate_weight[0], up_weight[0]], axis=1)
    in_own, in_rest = [jnp.pad(w, ((0, PAD), (0, 0))) for w in halves(w_in, 0)]
    down_own, down_rest = halves(down_weight[0], 1)
    tile, in_own, in_rest = lax.optimization_barrier((tile, in_own, in_rest))
    tiles = [tile]
    for step in (-1, 1, 2):
        tiles.append(move(tile, True, step))
    one = jnp.stack(tiles[:2], axis=0)
    two = jnp.stack(tiles[2:], axis=0)
    mine = [v.reshape(2 * rows, half + PAD) for v in ring_gather(one, two, False)]
    other = []
    for v in mine:
        other.append(swap(v))

    n = RING * RING * rows
    units = gate_weight.shape[2]

    def turned(v):
        return v.reshape(RING, RING, rows, v.shape[-1]).swapaxes(0, 1).reshape(n, v.shape[-1])

    def product(pieces, w):
        parts = []
        for v in pieces:
            parts.append(jnp.dot(v, w, preferred_element_type=jnp.float32))
        return jnp.concatenate(parts, axis=0)

    act_own = product(mine, in_own)
    act_rest = product(other, in_rest)
    act = act_own + turned(act_rest)
    hidden = (jax.nn.silu(act[:, :units]) * act[:, units:]).astype(jnp.bfloat16)
    hidden_rest = turned(hidden)

    lane = jnp.arange(PAD, dtype=jnp.int32)
    mask = (lane % 4 == expert) & (lane < 12)

    def scale_of(pieces):
        v = jnp.concatenate([p[:, half:] for p in pieces], axis=0)
        return jnp.sum(jnp.where(mask[None, :], v.astype(jnp.float32), 0.0), axis=1, keepdims=True)

    scale_own, scale_rest = scale_of(mine), scale_of(other)
    per = n // RING
    blocks = [None] * RING
    for d in (3, 1, 2, 0):
        span = slice(d * per, (d + 1) * per)
        rest = jnp.dot(hidden_rest[span], down_rest, preferred_element_type=jnp.float32) * scale_rest[span]
        came = swap(rest.astype(jnp.bfloat16))
        own = jnp.dot(hidden[span], down_own, preferred_element_type=jnp.float32) * scale_own[span]
        blocks[d] = add(own, came).astype(jnp.bfloat16).reshape(RING, rows, half)
    one, two = ring_reduce(blocks, False)
    from_far = move(two[1].astype(jnp.bfloat16), True, 2)
    from_left = move(one[1].astype(jnp.bfloat16), True, 1)
    from_right = move(two[0].astype(jnp.bfloat16), True, -1)
    last = add(one[0], from_left, from_far, from_right).astype(jnp.bfloat16)
    back = lax.all_to_all(last.reshape(16, tok_rows, half), ("c", "z"), split_axis=0, concat_axis=0, tiled=True)
    total = jnp.sum(back.reshape(2, 8, tok_rows, half).astype(jnp.float32), axis=1)
    return jnp.concatenate([total[0], total[1]], axis=1).astype(jnp.bfloat16)


def solution(mesh):
    fine = Mesh(mesh.devices.reshape(SIZES), AXES)
    expert, hidden = ("xl", "c"), ("y", "xh", "z")
    in_specs = (
        P(AXES, None),
        P(AXES, None),
        P(AXES, None),
        P(expert, None, hidden),
        P(expert, None, hidden),
        P(expert, hidden, None),
    )
    return jax.shard_map(shards, mesh=fine, in_specs=in_specs, out_specs=P(AXES, None), check_vma=False)
```

```python
import jax
import jax.numpy as jnp
from jax import lax
from jax.experimental import pallas as pl
from jax.experimental.pallas import tpu as pltpu
from jax.sharding import Mesh
from jax.sharding import PartitionSpec as P


AXES = ("xl", "c", "y", "xh", "z")
SIZES = (2, 2, 4, 2, 8)
RING = 4
PAD = 128


def flat(xl, c, y, xh, z):
    return (((xl * 2 + c) * 4 + y) * 2 + xh) * 8 + z


def ring_perm(first, step):
    pairs = []
    for c in range(2):
        along_x = (c == 0) == first
        for x in range(4):
            for y in range(4):
                for z in range(8):
                    tx, ty = ((x + step) % 4, y) if along_x else (x, (y + step) % 4)
                    pairs.append((flat(x % 2, c, y, x // 2, z), flat(tx % 2, c, ty, tx // 2, z)))
    return pairs


def move(v, first, step):
    return lax.ppermute(v, AXES, ring_perm(first, step))


def swap(v):
    return lax.ppermute(v, "c", [(0, 1), (1, 0)])


def ring_gather(one, two, first):
    from_left_one = move(one, first, 1)
    from_right_two = move(two, first, -1)
    from_left_two = move(two, first, 1)
    from_right_one = move(one, first, -1)
    far_one = move(from_left_one, first, 1)
    far_two = move(from_right_two, first, -1)
    return [one, two, from_right_one, from_right_two, from_left_one, from_left_two, far_one, far_two]


def add(*terms):
    total = terms[0].astype(jnp.float32)
    for term in terms[1:]:
        total = total + term.astype(jnp.float32)
    return total


def ring_reduce(blocks, first):
    own, right, left, far = blocks
    half = own.shape[0] // 2
    to_right = move(far[:half], first, 1)
    to_left = move(far[half:], first, -1)
    right_two = move(right[half:], first, 1)
    left_one = move(left[:half], first, -1)
    right_one = move(add(right[:half], to_right).astype(jnp.bfloat16), first, 1)
    left_two = move(add(left[half:], to_left).astype(jnp.bfloat16), first, -1)
    one = add(own[:half], right_one, left_one)
    two = add(own[half:], right_two, left_two)
    return one, two


def prepare_kernel(routing, weights, tokens, out):
    rows, width = tokens.shape
    half = width // 2
    lane = lax.broadcasted_iota(jnp.int32, (rows, PAD), 1)
    row = lax.broadcasted_iota(jnp.int32, (rows, PAD), 0)
    share = jnp.zeros((rows, PAD), jnp.float32)
    for t in range(rows):
        for k in range(2):
            here = (row == t) & (lane % 4 == routing[t, k])
            share = jnp.where(here, weights[t, k], share)
    high = share.astype(jnp.bfloat16).astype(jnp.float32)
    mid = (share - high).astype(jnp.bfloat16).astype(jnp.float32)
    low = share - high - mid
    extra = jnp.where(lane < 4, high, jnp.where(lane < 8, mid, jnp.where(lane < 12, low, 0.0)))
    extra = extra.astype(jnp.bfloat16)
    for core in range(2):
        side = tokens[:, core * half:(core + 1) * half]
        for copy in range(8):
            out[core * 8 + copy, :, :half] = side
            out[core * 8 + copy, :, half:] = extra


def prepare(tokens, routing, mix_weights):
    rows, width = tokens.shape
    return pl.pallas_call(
        prepare_kernel,
        out_shape=jax.ShapeDtypeStruct((16, rows, width // 2 + PAD), jnp.bfloat16),
        in_specs=[
            pl.BlockSpec(memory_space=pltpu.SMEM),
            pl.BlockSpec(memory_space=pltpu.SMEM),
            pl.BlockSpec(memory_space=pltpu.VMEM),
        ],
        out_specs=pl.BlockSpec(memory_space=pltpu.VMEM),
        name="prepare",
    )(routing, mix_weights, tokens)


def shards(tokens, routing, mix_weights, gate_weight, up_weight, down_weight):
    tok_rows, width = tokens.shape
    half = width // 2
    core = lax.axis_index("c")
    expert = lax.axis_index("xl") * 2 + core
    outgoing = prepare(tokens, routing, mix_weights)
    tile = lax.all_to_all(outgoing, ("c", "z"), split_axis=0, concat_axis=0, tiled=True)
    tile = tile.reshape(16 * tok_rows, half + PAD)
    rows = tile.shape[0]

    def halves(w, axis):
        own = lax.dynamic_slice_in_dim(w, core * half, half, axis)
        rest = lax.dynamic_slice_in_dim(w, (1 - core) * half, half, axis)
        return own, rest

    w_in = jnp.concatenate([gate_weight[0], up_weight[0]], axis=1)
    in_own, in_rest = halves(w_in, 0)
    down_own, down_rest = halves(down_weight[0], 1)
    tile, in_own, in_rest = lax.optimization_barrier((tile, in_own, in_rest))
    tiles = [tile]
    for step in (-1, 1, 2):
        tiles.append(move(tile, True, step))
    one = jnp.stack(tiles[:2], axis=0)
    two = jnp.stack(tiles[2:], axis=0)
    mine = [v.reshape(2 * rows, half + PAD) for v in ring_gather(one, two, False)]
    other = []
    for v in mine:
        other.append(swap(v))

    n = RING * RING * rows
    units = gate_weight.shape[2]

    def turned(v):
        return v.reshape(RING, RING, rows, v.shape[-1]).swapaxes(0, 1).reshape(n, v.shape[-1])

    def product(pieces, w):
        parts = []
        for v in pieces:
            parts.append(jnp.dot(v[:, :half], w, preferred_element_type=jnp.float32))
        return jnp.concatenate(parts, axis=0)

    act_own = product(mine, in_own)
    act_rest = product(other, in_rest)
    act = act_own + turned(act_rest)
    hidden = (jax.nn.silu(act[:, :units]) * act[:, units:]).astype(jnp.bfloat16)
    hidden_rest = turned(hidden)

    lane = jnp.arange(PAD, dtype=jnp.int32)
    mask = (lane % 4 == expert) & (lane < 12)

    def scale_of(pieces):
        v = jnp.concatenate([p[:, half:] for p in pieces], axis=0)
        return jnp.sum(jnp.where(mask[None, :], v.astype(jnp.float32), 0.0), axis=1, keepdims=True)

    scale_own, scale_rest = scale_of(mine), scale_of(other)
    per = n // RING
    blocks = [None] * RING
    for d in (3, 1, 2, 0):
        span = slice(d * per, (d + 1) * per)
        rest = jnp.dot(hidden_rest[span], down_rest, preferred_element_type=jnp.float32) * scale_rest[span]
        came = swap(rest.astype(jnp.bfloat16))
        own = jnp.dot(hidden[span], down_own, preferred_element_type=jnp.float32) * scale_own[span]
        blocks[d] = add(own, came).astype(jnp.bfloat16).reshape(RING, rows, half)
    one, two = ring_reduce(blocks, False)
    from_far = move(two[1].astype(jnp.bfloat16), True, 2)
    from_left = move(one[1].astype(jnp.bfloat16), True, 1)
    from_right = move(two[0].astype(jnp.bfloat16), True, -1)
    last = add(one[0], from_left, from_far, from_right).astype(jnp.bfloat16)
    back = lax.all_to_all(last.reshape(16, tok_rows, half), ("c", "z"), split_axis=0, concat_axis=0, tiled=True)
    total = jnp.sum(back.reshape(2, 8, tok_rows, half).astype(jnp.float32), axis=1)
    return jnp.concatenate([total[0], total[1]], axis=1).astype(jnp.bfloat16)


def solution(mesh):
    fine = Mesh(mesh.devices.reshape(SIZES), AXES)
    expert, hidden = ("xl", "c"), ("y", "xh", "z")
    in_specs = (
        P(AXES, None),
        P(AXES, None),
        P(AXES, None),
        P(expert, None, hidden),
        P(expert, None, hidden),
        P(expert, hidden, None),
    )
    return jax.shard_map(shards, mesh=fine, in_specs=in_specs, out_specs=P(AXES, None), check_vma=False)
```

```python
import jax
import jax.numpy as jnp
from jax import lax
from jax.experimental import pallas as pl
from jax.experimental.pallas import tpu as pltpu
from jax.sharding import Mesh
from jax.sharding import PartitionSpec as P


AXES = ("xl", "c", "y", "xh", "z")
SIZES = (2, 2, 4, 2, 8)
RING = 4
PAD = 128


def flat(xl, c, y, xh, z):
    return (((xl * 2 + c) * 4 + y) * 2 + xh) * 8 + z


def ring_perm(first, step):
    pairs = []
    for c in range(2):
        along_x = (c == 0) == first
        for x in range(4):
            for y in range(4):
                for z in range(8):
                    tx, ty = ((x + step) % 4, y) if along_x else (x, (y + step) % 4)
                    pairs.append((flat(x % 2, c, y, x // 2, z), flat(tx % 2, c, ty, tx // 2, z)))
    return pairs


def move(v, first, step):
    return lax.ppermute(v, AXES, ring_perm(first, step))


def swap(v):
    return lax.ppermute(v, "c", [(0, 1), (1, 0)])


def ring_gather(one, two, first):
    from_left_one = move(one, first, 1)
    from_right_two = move(two, first, -1)
    from_right_one = move(one, first, -1)
    from_left_two = move(two, first, 1)
    far_one = move(from_left_one, first, 1)
    far_two = move(from_right_two, first, -1)
    pairs = (one, two), (from_right_one, from_right_two), (from_left_one, from_left_two), (far_one, far_two)
    joined = []
    for pair in pairs:
        joined.append(jnp.concatenate(pair, axis=0))
    return joined


def add(*terms):
    total = terms[0].astype(jnp.float32)
    for term in terms[1:]:
        total = total + term.astype(jnp.float32)
    return total


def ring_reduce(blocks, first):
    own, right, left, far = blocks
    half = own.shape[0] // 2
    to_right = move(far[:half], first, 1)
    to_left = move(far[half:], first, -1)
    right_two = move(right[half:], first, 1)
    left_one = move(left[:half], first, -1)
    right_one = move(add(right[:half], to_right).astype(jnp.bfloat16), first, 1)
    left_two = move(add(left[half:], to_left).astype(jnp.bfloat16), first, -1)
    one = add(own[:half], right_one, left_one)
    two = add(own[half:], right_two, left_two)
    return one, two


def prepare_kernel(routing, weights, tokens, out):
    rows, width = tokens.shape
    half = width // 2
    lane = lax.broadcasted_iota(jnp.int32, (rows, PAD), 1)
    row = lax.broadcasted_iota(jnp.int32, (rows, PAD), 0)
    share = jnp.zeros((rows, PAD), jnp.float32)
    for t in range(rows):
        for k in range(2):
            here = (row == t) & (lane % 4 == routing[t, k])
            share = jnp.where(here, weights[t, k], share)
    high = share.astype(jnp.bfloat16).astype(jnp.float32)
    mid = (share - high).astype(jnp.bfloat16).astype(jnp.float32)
    low = share - high - mid
    extra = jnp.where(lane < 4, high, jnp.where(lane < 8, mid, jnp.where(lane < 12, low, 0.0)))
    extra = extra.astype(jnp.bfloat16)
    for core in range(2):
        side = tokens[:, core * half:(core + 1) * half]
        for copy in range(8):
            out[core * 8 + copy, :, :half] = side
            out[core * 8 + copy, :, half:] = extra


def prepare(tokens, routing, mix_weights):
    rows, width = tokens.shape
    return pl.pallas_call(
        prepare_kernel,
        out_shape=jax.ShapeDtypeStruct((16, rows, width // 2 + PAD), jnp.bfloat16),
        in_specs=[
            pl.BlockSpec(memory_space=pltpu.SMEM),
            pl.BlockSpec(memory_space=pltpu.SMEM),
            pl.BlockSpec(memory_space=pltpu.VMEM),
        ],
        out_specs=pl.BlockSpec(memory_space=pltpu.VMEM),
        name="prepare",
    )(routing, mix_weights, tokens)


def shards(tokens, routing, mix_weights, gate_weight, up_weight, down_weight):
    tok_rows, width = tokens.shape
    half = width // 2
    core = lax.axis_index("c")
    expert = lax.axis_index("xl") * 2 + core
    outgoing = prepare(tokens, routing, mix_weights)
    tile = lax.all_to_all(outgoing, ("c", "z"), split_axis=0, concat_axis=0, tiled=True)
    tile = tile.reshape(16 * tok_rows, half + PAD)
    rows = tile.shape[0]

    def halves(w, axis):
        own = lax.dynamic_slice_in_dim(w, core * half, half, axis)
        rest = lax.dynamic_slice_in_dim(w, (1 - core) * half, half, axis)
        return own, rest

    w_in = jnp.concatenate([gate_weight[0], up_weight[0]], axis=1)
    in_own, in_rest = halves(w_in, 0)
    down_own, down_rest = halves(down_weight[0], 1)
    tile, in_own, in_rest = lax.optimization_barrier((tile, in_own, in_rest))
    tiles = [tile]
    for step in (-1, 1, 2):
        tiles.append(move(tile, True, step))
    one = jnp.stack(tiles[:2], axis=0)
    two = jnp.stack(tiles[2:], axis=0)
    mine = [v.reshape(RING * rows, half + PAD) for v in ring_gather(one, two, False)]
    other = []
    for v in mine:
        other.append(swap(v))

    n = RING * RING * rows
    units = gate_weight.shape[2]

    def turned(v):
        return v.reshape(RING, RING, rows, v.shape[-1]).swapaxes(0, 1).reshape(n, v.shape[-1])

    def product(pieces, w):
        parts = []
        for v in pieces:
            parts.append(jnp.dot(v[:, :half], w, preferred_element_type=jnp.float32))
        return jnp.concatenate(parts, axis=0)

    act_own = product(mine, in_own)
    act_rest = product(other, in_rest)
    act = act_own + turned(act_rest)
    hidden = (jax.nn.silu(act[:, :units]) * act[:, units:]).astype(jnp.bfloat16)
    hidden_rest = turned(hidden)

    lane = jnp.arange(PAD, dtype=jnp.int32)
    mask = (lane % 4 == expert) & (lane < 12)

    def scale_of(pieces):
        v = jnp.concatenate([p[:, half:] for p in pieces], axis=0)
        return jnp.sum(jnp.where(mask[None, :], v.astype(jnp.float32), 0.0), axis=1, keepdims=True)

    scale_own, scale_rest = scale_of(mine), scale_of(other)
    per = n // RING
    blocks = [None] * RING
    for d in (3, 1, 2, 0):
        span = slice(d * per, (d + 1) * per)
        rest = jnp.dot(hidden_rest[span], down_rest, preferred_element_type=jnp.float32) * scale_rest[span]
        came = swap(rest.astype(jnp.bfloat16))
        own = jnp.dot(hidden[span], down_own, preferred_element_type=jnp.float32) * scale_own[span]
        blocks[d] = add(own, came).astype(jnp.bfloat16).reshape(RING, rows, half)
    one, two = ring_reduce(blocks, False)
    from_far = move(two[1].astype(jnp.bfloat16), True, 2)
    from_left = move(one[1].astype(jnp.bfloat16), True, 1)
    from_right = move(two[0].astype(jnp.bfloat16), True, -1)
    last = add(one[0], from_left, from_far, from_right).astype(jnp.bfloat16)
    back = lax.all_to_all(last.reshape(16, tok_rows, half), ("c", "z"), split_axis=0, concat_axis=0, tiled=True)
    total = jnp.sum(back.reshape(2, 8, tok_rows, half).astype(jnp.float32), axis=1)
    return jnp.concatenate([total[0], total[1]], axis=1).astype(jnp.bfloat16)


def solution(mesh):
    fine = Mesh(mesh.devices.reshape(SIZES), AXES)
    expert, hidden = ("xl", "c"), ("y", "xh", "z")
    in_specs = (
        P(AXES, None),
        P(AXES, None),
        P(AXES, None),
        P(expert, None, hidden),
        P(expert, None, hidden),
        P(expert, hidden, None),
    )
    return jax.shard_map(shards, mesh=fine, in_specs=in_specs, out_specs=P(AXES, None), check_vma=False)
```
